32 devices in a mesh: gx: 8 (over y, x, core), gy: 4 (over z).
Axes of the slice: x: 2, y: 2, z: 4, core: 2. Of those that a mesh axis runs over, the one named last changes fastest.
Arguments:
- field: bfloat16 [64, 16, 64, 1024], P('gy', None, None, 'gx'), may hold values from -6 to 6
- conv_w: bfloat16 [27, 64, 64], replicated, may hold values from -0.15625 to 0.15625
- spec_re: float32 [16, 64, 64], replicated, may hold values from -6 to 6
- spec_im: float32 [16, 64, 64], replicated, may hold values from -6 to 6
- mlp_in: bfloat16 [256, 64], replicated, may hold values from -0.75 to 0.75
- mlp_out: bfloat16 [64, 256], replicated, may hold values from -0.375 to 0.375
Outputs:
- result: bfloat16 [64, 16, 64, 1024], P('gy', None, None, 'gx')
The draws below stay inside these ranges and needn't reach their ends.
All inputs are finite; a program needn't handle non-finite values.
Results may differ from the reference program's by a relative error of at most 0.0062.
Values may be sent and summed in bfloat16 or wider, within the bound.
A program may use at most 128 MiB of HBM per device.

```python
import math
import jax
import jax.numpy as jnp
from jax import lax

C = 64
HID = 256
MODES = 16
NZ = 16
NX = 1024
NY = 64


def block_levels(rng, dims, shards, least, top_value):
    def one(axis_at, parts):
        heights = jax.random.uniform(jax.random.fold_in(jax.random.fold_in(rng, 6), axis_at), (parts,), jnp.float32, least / len(shards), top_value / len(shards))
        return jnp.repeat(jnp.exp(heights), dims[axis_at] // parts).reshape((-1,) + (1,) * (len(dims) - axis_at - 1))

    loudness = one(*shards[0])
    for cut in shards[1:]:
        loudness = loudness * one(*cut)
    return loudness


def scatter_about(rng, dims, deviation, reach, split=(), held_as=jnp.bfloat16):
    factor_of = block_levels(rng, dims, split, -0.22, 0.18) if split else 1.0
    array = jax.random.normal(rng, dims, jnp.float32) * deviation * factor_of
    return jnp.minimum(jnp.maximum(array, -reach), reach).astype(held_as)


def setup_inputs(seed: int = 0) -> dict:
    arg_keys = jax.random.split(jax.random.key(seed), 7)
    field = scatter_about(arg_keys[0], (NY, NZ, C, NX), 1.0, 6.0, ((0, 4), (3, 8)))
    conv_w = scatter_about(arg_keys[1], (27, C, C), (27 * C) ** -0.5, 0.15625)
    spec_re = scatter_about(arg_keys[2], (MODES, C, C), 1.0, 6.0, (), jnp.float32)
    spec_im = scatter_about(arg_keys[3], (MODES, C, C), 1.0, 6.0, (), jnp.float32)
    mlp_in = scatter_about(arg_keys[4], (HID, C), C ** -0.5, 0.75)
    mlp_out = scatter_about(arg_keys[5], (C, HID), HID ** -0.5, 0.375)
    return {"field": field, "conv_w": conv_w, "spec_re": spec_re, "spec_im": spec_im, "mlp_in": mlp_in, "mlp_out": mlp_out}


def forward_table(start, count, total, modes):
    places = start + jnp.arange(count, dtype=jnp.int32)
    orders = jnp.arange(modes, dtype=jnp.int32)
    phase = (places[:, None] * orders[None, :]) % total
    angle = phase.astype(jnp.float32) * (2.0 * math.pi / total)
    return jnp.concatenate([jnp.cos(angle), -jnp.sin(angle)], axis=1).astype(jnp.bfloat16)


def inverse_table(start, count, total, modes):
    places = start + jnp.arange(count, dtype=jnp.int32)
    orders = jnp.arange(modes, dtype=jnp.int32)
    phase = (orders[:, None] * places[None, :]) % total
    angle = phase.astype(jnp.float32) * (2.0 * math.pi / total)
    scales = jnp.where(orders == 0, 1.0, 2.0).astype(jnp.float32) / total
    return jnp.concatenate([jnp.cos(angle) * scales[:, None], -jnp.sin(angle) * scales[:, None]], axis=0)


def mix_modes(spectrum, spec_re, spec_im):
    modes = spec_re.shape[0]
    real_part = spectrum[..., :modes]
    imag_part = spectrum[..., modes:]
    highest = lax.Precision.HIGHEST
    out_real = jnp.einsum("koc,...ck->...ok", spec_re, real_part, precision=highest) - jnp.einsum("koc,...ck->...ok", spec_im, imag_part, precision=highest)
    out_imag = jnp.einsum("koc,...ck->...ok", spec_re, imag_part, precision=highest) + jnp.einsum("koc,...ck->...ok", spec_im, real_part, precision=highest)
    return jnp.concatenate([out_real, out_imag], axis=-1)


def lift(field, conv_w):
    depth = field.shape[1]
    width = field.shape[3]
    padded = jnp.pad(field, ((1, 1), (1, 1), (0, 0), (1, 1)))
    weights = conv_w.astype(jnp.float32)

    def one_row(row_index):
        slab = lax.dynamic_slice_in_dim(padded, row_index, 3, 0).astype(jnp.float32)
        total = lax.dynamic_index_in_dim(field, row_index, 0, keepdims=False).astype(jnp.float32)
        for shift_y in range(3):
            for shift_z in range(3):
                for shift_x in range(3):
                    tap_index = (shift_y * 3 + shift_z) * 3 + shift_x
                    window = slab[shift_y, shift_z:shift_z + depth, :, shift_x:shift_x + width]
                    total = total + jnp.einsum("oc,zcx->zox", weights[tap_index], window)
        return total.astype(jnp.bfloat16)

    return lax.map(one_row, jnp.arange(field.shape[0], dtype=jnp.int32))


def reference(field, conv_w, spec_re, spec_im, mlp_in, mlp_out):
    lifted = lift(field, conv_w)
    forward = forward_table(0, NX, NX, MODES)
    spectrum = jnp.dot(lifted, forward, preferred_element_type=jnp.float32)
    mixed = mix_modes(spectrum, spec_re, spec_im)
    inverse = inverse_table(0, NX, NX, MODES)
    first_w = mlp_in.astype(jnp.float32)
    second_w = mlp_out.astype(jnp.float32)

    def finish(row_index):
        mixed_row = lax.dynamic_index_in_dim(mixed, row_index, 0, keepdims=False)
        lifted_row = lax.dynamic_index_in_dim(lifted, row_index, 0, keepdims=False)
        branch = jnp.dot(mixed_row, inverse, precision=lax.Precision.HIGHEST)
        blended = (lifted_row.astype(jnp.float32) + branch).astype(jnp.bfloat16)
        hidden = jax.nn.gelu(jnp.einsum("hc,zcx->zhx", first_w, blended.astype(jnp.float32))).astype(jnp.bfloat16)
        down = jnp.einsum("ch,zhx->zcx", second_w, hidden.astype(jnp.float32))
        return (blended.astype(jnp.float32) + down).astype(jnp.bfloat16)

    return lax.map(finish, jnp.arange(NY, dtype=jnp.int32))
```

```python
import functools
import math

import jax
import jax.numpy as jnp
from jax import lax
from jax.experimental import pallas as pl
from jax.experimental.pallas import tpu as pltpu
from jax.sharding import PartitionSpec as P

F32 = jnp.float32
BF16 = jnp.bfloat16
MESH = pl.DeviceIdType.MESH
CHUNKS = 4
NT = (((1,), (1,)), ((), ()))
TN = (((0,), (0,)), ((), ()))


def kernel(
    n, m, field, conv_w, spec_re, spec_im, mlp_in, mlp_out, out,
    xs, lifted, halo_out, halo_in, halo_top, halo_bot, toep, mixw, fwd, inv,
    part, got, tsum, mixed,
    load_sem, store_sem, row_send, row_recv, side_send, side_recv, corner_send, corner_recv,
    rs_send, rs_recv, ag_send, ag_recv,
):
    rows, depth, ch, width = field.shape
    modes = spec_re.shape[0]
    total = n * width
    pairs = depth // 2
    crows = rows // CHUNKS
    cpairs = crows * pairs
    share = cpairs // n
    per = width // depth
    groups = rows // per
    me = lax.axis_index("gx")
    my = lax.axis_index("gy")
    has_left, has_right = me > 0, me < n - 1
    has_up, has_down = my > 0, my < m - 1

    def load(y):
        return pltpu.make_async_copy(
            field.at[y], xs.at[1, y + 1, pl.ds(1, depth)], load_sem.at[y]
        )

    @pl.loop(0, rows)
    def _(y):
        load(y).start()

    barrier = pltpu.get_barrier_semaphore()

    @pl.loop(1, n)
    def _(o):
        pl.semaphore_signal(
            barrier, inc=1, device_id={"gx": lax.rem(me + o, n)}, device_id_type=MESH
        )

    @pl.when(has_up)
    def _():
        pl.semaphore_signal(barrier, inc=1, device_id={"gy": my - 1}, device_id_type=MESH)

    @pl.when(has_down)
    def _():
        pl.semaphore_signal(barrier, inc=1, device_id={"gy": my + 1}, device_id_type=MESH)

    pl.semaphore_wait(barrier, n - 1 + has_up.astype(jnp.int32) + has_down.astype(jnp.int32))

    def row_up():
        return pltpu.make_async_remote_copy(
            src_ref=field.at[0], dst_ref=xs.at[1, rows + 1, pl.ds(1, depth)],
            send_sem=row_send.at[0], recv_sem=row_recv.at[0],
            device_id={"gy": my - 1}, device_id_type=MESH,
        )

    def row_down():
        return pltpu.make_async_remote_copy(
            src_ref=field.at[rows - 1], dst_ref=xs.at[1, 0, pl.ds(1, depth)],
            send_sem=row_send.at[1], recv_sem=row_recv.at[1],
            device_id={"gy": my + 1}, device_id_type=MESH,
        )

    pl.when(has_up)(lambda: row_up().start())
    pl.when(has_down)(lambda: row_down().start())

    lane = lax.broadcasted_iota(jnp.int32, (ch, width), 1)

    for g in range(groups):
        for y in range(g * per, (g + 1) * per):
            load(y).wait()
        first = jnp.zeros((ch, width), BF16)
        last = jnp.zeros((ch, width), BF16)
        for y in range(per):
            for z in range(depth):
                tile = xs[1, g * per + y + 1, z + 1]
                to = y * depth + z
                first = jnp.where(lane == to, tile if to == 0 else pltpu.roll(tile, to, 1), first)
                back = (to + 1) % width
                last = jnp.where(lane == to, tile if back == 0 else pltpu.roll(tile, back, 1), last)
        halo_out[0, g] = first
        halo_out[1, g] = last

    def side_left(g):
        return pltpu.make_async_remote_copy(
            src_ref=halo_out.at[0, g], dst_ref=halo_in.at[g, 1],
            send_sem=side_send.at[0, g], recv_sem=side_recv.at[1, g],
            device_id={"gx": me - 1}, device_id_type=MESH,
        )

    def side_right(g):
        return pltpu.make_async_remote_copy(
            src_ref=halo_out.at[1, g], dst_ref=halo_in.at[g, 0],
            send_sem=side_send.at[1, g], recv_sem=side_recv.at[0, g],
            device_id={"gx": me + 1}, device_id_type=MESH,
        )

    for g in range(groups):
        pl.when(has_left)(lambda g=g: side_left(g).start())
        pl.when(has_right)(lambda g=g: side_right(g).start())

    blank = jnp.zeros((ch, width), BF16)

    @pl.loop(0, rows + 2)
    def _(y):
        for d in range(3):
            xs[d, y, 0] = blank
            xs[d, y, depth + 1] = blank

    @pl.when(jnp.logical_not(has_up))
    def _():
        for z in range(depth):
            xs[1, 0, z + 1] = blank
        for s in range(2):
            halo_top[s] = blank

    @pl.when(jnp.logical_not(has_down))
    def _():
        for z in range(depth):
            xs[1, rows + 1, z + 1] = blank
        for s in range(2):
            halo_bot[s] = blank

    @pl.when(jnp.logical_not(has_left))
    def _():
        for g in range(groups):
            halo_in[g, 0] = blank

    @pl.when(jnp.logical_not(has_right))
    def _():
        for g in range(groups):
            halo_in[g, 1] = blank

    square = jnp.zeros((ch, ch), BF16)
    for a in range(3):
        for d in range(3):
            t = a * 3 + d
            taps = [conv_w[(a * 3 + b) * 3 + d] for b in range(3)]
            cols = pl.ds(t * 4 * ch, 4 * ch)
            toep[0:ch, cols] = jnp.concatenate(taps + [square], axis=1)
            toep[ch:2 * ch, cols] = jnp.concatenate([square] + taps, axis=1)

    @pl.loop(0, modes)
    def _(k):
        re = spec_re[k].astype(BF16)
        im = spec_im[k].astype(BF16)
        neg = -im
        mixw[k, 0:ch] = jnp.concatenate([re, square, neg, square], axis=1)
        mixw[k, ch:2 * ch] = jnp.concatenate([square, re, square, neg], axis=1)
        mixw[k, 2 * ch:3 * ch] = jnp.concatenate([im, square, re, square], axis=1)
        mixw[k, 3 * ch:4 * ch] = jnp.concatenate([square, im, square, re], axis=1)

    places = me * width + lax.broadcasted_iota(jnp.int32, (modes, width), 1)
    orders = lax.broadcasted_iota(jnp.int32, (modes, width), 0)
    angle = lax.rem(places * orders, total).astype(F32) * (2.0 * math.pi / total)
    cosine, sine = jnp.cos(angle), -jnp.sin(angle)
    fwd[...] = jnp.concatenate([cosine, sine], axis=0).astype(BF16)
    scales = jnp.where(orders == 0, 1.0, 2.0).astype(F32) / total
    table = jnp.concatenate([cosine * scales, sine * scales], axis=0)
    high = table.astype(BF16)
    inv[0:2 * modes] = high
    inv[2 * modes:4 * modes] = (table - high.astype(F32)).astype(BF16)

    for g in range(groups):
        pl.when(has_left)(lambda g=g: side_right(g).wait_recv())
        pl.when(has_right)(lambda g=g: side_left(g).wait_recv())

    def corner_up():
        return pltpu.make_async_remote_copy(
            src_ref=halo_in.at[0], dst_ref=halo_bot,
            send_sem=corner_send.at[0], recv_sem=corner_recv.at[0],
            device_id={"gy": my - 1}, device_id_type=MESH,
        )

    def corner_down():
        return pltpu.make_async_remote_copy(
            src_ref=halo_in.at[groups - 1], dst_ref=halo_top,
            send_sem=corner_send.at[1], recv_sem=corner_recv.at[1],
            device_id={"gy": my + 1}, device_id_type=MESH,
        )

    pl.when(has_up)(lambda: corner_up().start())
    pl.when(has_down)(lambda: corner_down().start())

    def shift_row(y, left, right):
        for z in range(depth):
            tile = xs[1, y, z + 1]
            edge = left if z == 0 else pltpu.roll(left, width - z, 1)
            xs[0, y, z + 1] = jnp.where(lane == 0, edge, pltpu.roll(tile, 1, 1))
            xs[2, y, z + 1] = jnp.where(
                lane == width - 1,
                pltpu.roll(right, width - 1 - z, 1),
                pltpu.roll(tile, width - 1, 1),
            )

    def shift_own(y):
        g = y // per
        turn = lax.rem(width - lax.rem(y, per) * depth, width)
        shift_row(y + 1, pltpu.roll(halo_in[g, 0], turn, 1), pltpu.roll(halo_in[g, 1], turn, 1))

    def lift_row(y):
        for q in range(depth // 4):
            blocks = []
            for a in range(3):
                for d in range(3):
                    one = xs[d, y + a, pl.ds(4 * q, 4)].reshape(4 * ch, width)
                    two = xs[d, y + a, pl.ds(4 * q + 2, 4)].reshape(4 * ch, width)
                    blocks.append(jnp.concatenate([one, two], axis=1))
            acc = jnp.dot(toep[...], jnp.concatenate(blocks, axis=0), preferred_element_type=F32)
            for p in range(2):
                own = xs[1, y + 1, pl.ds(4 * q + 2 * p + 1, 2)].reshape(2 * ch, width)
                new = (own.astype(F32) + acc[:, p * width:(p + 1) * width]).astype(BF16)
                lifted[y, 2 * q + p] = new
                modes_part = lax.dot_general(fwd[...], new, NT, preferred_element_type=F32)
                part[y * pairs + 2 * q + p] = modes_part.astype(BF16)

    def rs_copy(c, o):
        to = lax.rem(me + o, n)
        return pltpu.make_async_remote_copy(
            src_ref=part.at[pl.ds(c * cpairs + to * share, share)], dst_ref=got.at[c, o],
            send_sem=rs_send.at[c, o], recv_sem=rs_recv.at[c, o],
            device_id={"gx": to}, device_id_type=MESH,
        )

    def ag_copy(c, o):
        mine = pl.ds(c * cpairs + me * share, share)
        return pltpu.make_async_remote_copy(
            src_ref=mixed.at[mine], dst_ref=mixed.at[mine],
            send_sem=ag_send.at[c, o], recv_sem=ag_recv.at[c, o],
            device_id={"gx": lax.rem(me + o, n)}, device_id_type=MESH,
        )

    def ag_wait(c, o):
        theirs = pl.ds(c * cpairs + lax.rem(me + n - o, n) * share, share)
        pltpu.make_async_remote_copy(
            src_ref=mixed.at[theirs], dst_ref=mixed.at[theirs],
            send_sem=ag_send.at[c, o], recv_sem=ag_recv.at[c, o],
            device_id={"gx": lax.rem(me + o, n)}, device_id_type=MESH,
        ).wait_recv()

    def lift_chunk(c):
        pl.loop(c * crows, (c + 1) * crows)(lift_row)
        pl.loop(1, n)(lambda o: rs_copy(c, o).start())

    def mix_chunk(c):
        mine = pl.ds(c * cpairs + me * share, share)
        tsum[...] = part[mine].astype(F32)

        @pl.loop(1, n)
        def _(o):
            rs_copy(c, o).wait_recv()
            tsum[...] += got[c, o].astype(F32)

        for k in range(modes):
            data = jnp.concatenate([tsum[:, k, :], tsum[:, modes + k, :]], axis=1)
            top = data.astype(BF16).astype(F32)
            lhs = jnp.concatenate([top, data - top], axis=0).astype(BF16)
            both = lax.dot_general(lhs, mixw[k], NT, preferred_element_type=F32)
            new = both[0:share] + both[share:2 * share]
            tsum[:, k, :] = new[:, :width]
            tsum[:, modes + k, :] = new[:, width:]
        mixed[mine] = tsum[...].astype(BF16)
        pl.loop(1, n)(lambda o: ag_copy(c, o).start())

    def store(y):
        return pltpu.make_async_copy(lifted.at[y], out.at[y], store_sem.at[y])

    slope = math.sqrt(2.0 / math.pi)

    def finish_row(y):
        for p in range(pairs):
            spec = mixed[y * pairs + p]
            branch = lax.dot_general(
                jnp.concatenate([spec, spec], axis=0), inv[...], TN, preferred_element_type=F32
            )
            blended = (lifted[y, p].astype(F32) + branch).astype(BF16)
            wide = jnp.concatenate([blended[0:ch], blended[ch:2 * ch]], axis=1)
            h = jnp.dot(mlp_in[...], wide, preferred_element_type=F32)
            h = h * (0.5 + 0.5 * jnp.tanh(h * (slope + (slope * 0.044715) * (h * h))))
            down = jnp.dot(mlp_out[...], h.astype(BF16), preferred_element_type=F32)
            res = (wide.astype(F32) + down).astype(BF16)
            lifted[y, p] = jnp.concatenate([res[:, :width], res[:, width:]], axis=0)
        store(y).start()

    def finish_chunk(c):
        pl.loop(1, n)(lambda o: ag_wait(c, o))
        pl.loop(c * crows, (c + 1) * crows)(finish_row)

    pl.loop(0, rows)(shift_own)
    inner = list(range(1, CHUNKS - 1))
    for c in inner:
        lift_chunk(c)
    mix_chunk(inner[0])

    pl.when(has_up)(lambda: row_down().wait_recv())
    pl.when(has_up)(lambda: corner_down().wait_recv())
    turn = width - (per - 1) * depth
    shift_row(0, pltpu.roll(halo_top[0], turn, 1), pltpu.roll(halo_top[1], turn, 1))
    lift_chunk(0)
    for c in inner[1:]:
        mix_chunk(c)
    pl.when(has_down)(lambda: row_up().wait_recv())
    pl.when(has_down)(lambda: corner_up().wait_recv())
    shift_row(rows + 1, halo_bot[0], halo_bot[1])
    lift_chunk(CHUNKS - 1)
    mix_chunk(0)
    finish_chunk(inner[0])
    mix_chunk(CHUNKS - 1)
    for c in inner[1:] + [0, CHUNKS - 1]:
        finish_chunk(c)

    pl.loop(0, rows)(lambda y: store(y).wait())
    pl.when(has_up)(lambda: row_up().wait_send())
    pl.when(has_down)(lambda: row_down().wait_send())
    pl.when(has_up)(lambda: corner_up().wait_send())
    pl.when(has_down)(lambda: corner_down().wait_send())
    for g in range(groups):
        pl.when(has_left)(lambda g=g: side_left(g).wait_send())
        pl.when(has_right)(lambda g=g: side_right(g).wait_send())
    for c in range(CHUNKS):
        @pl.loop(1, n)
        def _(o):
            rs_copy(c, o).wait_send()
            ag_copy(c, o).wait_send()


def per_device(n, m, field, conv_w, spec_re, spec_im, mlp_in, mlp_out):
    rows, depth, ch, width = field.shape
    modes = spec_re.shape[0]
    pairs = depth // 2
    cpairs = rows // CHUNKS * pairs
    share = cpairs // n
    groups = rows * depth // width
    dma = pltpu.SemaphoreType.DMA
    vmem = pl.BlockSpec(memory_space=pltpu.VMEM)
    result = pl.pallas_call(
        functools.partial(kernel, n, m),
        out_shape=jax.ShapeDtypeStruct((rows, pairs, 2 * ch, width), BF16),
        in_specs=[pl.BlockSpec(memory_space=pl.ANY)] + [vmem] * 5,
        out_specs=pl.BlockSpec(memory_space=pl.ANY),
        scratch_shapes=[
            pltpu.VMEM((3, rows + 2, depth + 2, ch, width), BF16),
            pltpu.VMEM((rows, pairs, 2 * ch, width), BF16),
            pltpu.VMEM((2, groups, ch, width), BF16),
            pltpu.VMEM((groups, 2, ch, width), BF16),
            pltpu.VMEM((2, ch, width), BF16),
            pltpu.VMEM((2, ch, width), BF16),
            pltpu.VMEM((2 * ch, 36 * ch), BF16),
            pltpu.VMEM((modes, 4 * ch, 4 * ch), BF16),
            pltpu.VMEM((2 * modes, width), BF16),
            pltpu.VMEM((4 * modes, width), BF16),
            pltpu.VMEM((rows * pairs, 2 * modes, width), BF16),
            pltpu.VMEM((CHUNKS, n, share, 2 * modes, width), BF16),
            pltpu.VMEM((share, 2 * modes, width), F32),
            pltpu.VMEM((rows * pairs, 2 * modes, width), BF16),
            dma((rows,)), dma((rows,)),
            dma((2,)), dma((2,)),
            dma((2, groups)), dma((2, groups)),
            dma((2,)), dma((2,)),
            dma((CHUNKS, n)), dma((CHUNKS, n)),
            dma((CHUNKS, n)), dma((CHUNKS, n)),
        ],
        compiler_params=pltpu.CompilerParams(
            collective_id=0, has_side_effects=True, vmem_limit_bytes=56 << 20
        ),
    )(field, conv_w, spec_re, spec_im, mlp_in, mlp_out)
    return result.reshape(rows, depth, ch, width)


def solution(mesh):
    in_specs = (P("gy", None, None, "gx"), P(), P(), P(), P(), P())
    out_specs = P("gy", None, None, "gx")
    return jax.shard_map(
        functools.partial(per_device, mesh.shape["gx"], mesh.shape["gy"]),
        mesh=mesh, in_specs=in_specs, out_specs=out_specs, check_vma=False,
    )
```

```python
import functools
import math

import jax
import jax.numpy as jnp
from jax import lax
from jax.experimental import pallas as pl
from jax.experimental.pallas import tpu as pltpu
from jax.sharding import PartitionSpec as P

F32 = jnp.float32
BF16 = jnp.bfloat16
MESH = pl.DeviceIdType.MESH
CHUNKS = 4
NT = (((1,), (1,)), ((), ()))
TN = (((0,), (0,)), ((), ()))


def kernel(
    n, m, field, conv_w, spec_re, spec_im, mlp_in, mlp_out, out,
    xs, shifted, carry_a, carry_b, lifted, halo_out, halo_in, up_w, down_w, toep, mixw, fwd, inv,
    part, got, tsum, mixed,
    load_sem, row_send, row_recv, side_send, side_recv, corner_send, corner_recv,
    rs_send, rs_recv, ag_send, ag_recv,
):
    rows, depth, ch, width = field.shape
    modes = spec_re.shape[0]
    total = n * width
    pairs = depth // 2
    crows = rows // CHUNKS
    cpairs = crows * pairs
    share = cpairs // n
    per = width // depth
    groups = rows // per
    me = lax.axis_index("gx")
    my = lax.axis_index("gy")
    has_left, has_right = me > 0, me < n - 1
    has_up, has_down = my > 0, my < m - 1

    def load(y):
        return pltpu.make_async_copy(
            field.at[y], xs.at[y + 1, pl.ds(1, depth)], load_sem.at[y]
        )

    @pl.loop(0, rows)
    def _(y):
        load(y).start()

    barrier = pltpu.get_barrier_semaphore()

    @pl.loop(1, n)
    def _(o):
        pl.semaphore_signal(
            barrier, inc=1, device_id={"gx": lax.rem(me + o, n)}, device_id_type=MESH
        )

    @pl.when(has_up)
    def _():
        pl.semaphore_signal(barrier, inc=1, device_id={"gy": my - 1}, device_id_type=MESH)

    @pl.when(has_down)
    def _():
        pl.semaphore_signal(barrier, inc=1, device_id={"gy": my + 1}, device_id_type=MESH)

    pl.semaphore_wait(barrier, n - 1 + has_up.astype(jnp.int32) + has_down.astype(jnp.int32))

    def row_up():
        return pltpu.make_async_remote_copy(
            src_ref=field.at[0], dst_ref=xs.at[rows + 1, pl.ds(1, depth)],
            send_sem=row_send.at[0], recv_sem=row_recv.at[0],
            device_id={"gy": my - 1}, device_id_type=MESH,
        )

    def row_down():
        return pltpu.make_async_remote_copy(
            src_ref=field.at[rows - 1], dst_ref=xs.at[0, pl.ds(1, depth)],
            send_sem=row_send.at[1], recv_sem=row_recv.at[1],
            device_id={"gy": my + 1}, device_id_type=MESH,
        )

    pl.when(has_up)(lambda: row_up().start())
    pl.when(has_down)(lambda: row_down().start())

    lane = lax.broadcasted_iota(jnp.int32, (ch, width), 1)

    for g in range(groups):
        for y in range(g * per, (g + 1) * per):
            load(y).wait()
        first = jnp.zeros((ch, width), BF16)
        last = jnp.zeros((ch, width), BF16)
        for y in range(per):
            for z in range(depth):
                tile = xs[g * per + y + 1, z + 1]
                to = y * depth + z
                first = jnp.where(lane == to, tile if to == 0 else pltpu.roll(tile, to, 1), first)
                back = (to + 1) % width
                last = jnp.where(lane == to, tile if back == 0 else pltpu.roll(tile, back, 1), last)
        halo_out[0, g] = first
        halo_out[1, g] = last

    def side_left(g):
        return pltpu.make_async_remote_copy(
            src_ref=halo_out.at[0, g], dst_ref=halo_in.at[g + 1, 1],
            send_sem=side_send.at[0, g], recv_sem=side_recv.at[1, g],
            device_id={"gx": me - 1}, device_id_type=MESH,
        )

    def side_right(g):
        return pltpu.make_async_remote_copy(
            src_ref=halo_out.at[1, g], dst_ref=halo_in.at[g + 1, 0],
            send_sem=side_send.at[1, g], recv_sem=side_recv.at[0, g],
            device_id={"gx": me + 1}, device_id_type=MESH,
        )

    for g in range(groups):
        pl.when(has_left)(lambda g=g: side_left(g).start())
        pl.when(has_right)(lambda g=g: side_right(g).start())

    blank = jnp.zeros((ch, width), BF16)

    @pl.loop(0, rows + 2)
    def _(y):
        xs[y, 0] = blank
        xs[y, depth + 1] = blank

    for d in range(2):
        shifted[d, 0] = blank
        shifted[d, depth + 1] = blank

    @pl.when(jnp.logical_not(has_up))
    def _():
        for z in range(depth):
            xs[0, z + 1] = blank
        for s in range(2):
            halo_in[0, s] = blank

    @pl.when(jnp.logical_not(has_down))
    def _():
        for z in range(depth):
            xs[rows + 1, z + 1] = blank
        for s in range(2):
            halo_in[groups + 1, s] = blank

    @pl.when(jnp.logical_not(has_left))
    def _():
        for g in range(groups):
            halo_in[g + 1, 0] = blank

    @pl.when(jnp.logical_not(has_right))
    def _():
        for g in range(groups):
            halo_in[g + 1, 1] = blank

    up_w[...] = mlp_in[...].astype(F32).T.astype(BF16)
    down_w[...] = mlp_out[...] * jnp.asarray(0.5, BF16)

    square = jnp.zeros((ch, ch), BF16)
    for a in range(3):
        for d in range(3):
            taps = [conv_w[(a * 3 + b) * 3 + d] for b in range(3)]
            cols = pl.ds(d * 4 * ch, 4 * ch)
            toep[pl.ds(2 * a * ch, ch), cols] = jnp.concatenate(taps + [square], axis=1)
            toep[pl.ds((2 * a + 1) * ch, ch), cols] = jnp.concatenate([square] + taps, axis=1)

    @pl.loop(0, modes)
    def _(k):
        re = spec_re[k].astype(BF16)
        im = spec_im[k].astype(BF16)
        neg = -im
        mixw[k, 0:ch] = jnp.concatenate([re, square, neg, square], axis=1)
        mixw[k, ch:2 * ch] = jnp.concatenate([square, re, square, neg], axis=1)
        mixw[k, 2 * ch:3 * ch] = jnp.concatenate([im, square, re, square], axis=1)
        mixw[k, 3 * ch:4 * ch] = jnp.concatenate([square, im, square, re], axis=1)

    places = me * width + lax.broadcasted_iota(jnp.int32, (modes, width), 1)
    orders = lax.broadcasted_iota(jnp.int32, (modes, width), 0)
    angle = lax.rem(places * orders, total).astype(F32) * (2.0 * math.pi / total)
    cosine, sine = jnp.cos(angle), -jnp.sin(angle)
    fwd[...] = jnp.concatenate([cosine, sine], axis=0).astype(BF16)
    scales = jnp.where(orders == 0, 1.0, 2.0).astype(F32) / total
    table = jnp.concatenate([cosine * scales, sine * scales], axis=0)
    high = table.astype(BF16)
    inv[0:2 * modes] = high
    inv[2 * modes:4 * modes] = (table - high.astype(F32)).astype(BF16)

    for g in range(groups):
        pl.when(has_left)(lambda g=g: side_right(g).wait_recv())
        pl.when(has_right)(lambda g=g: side_left(g).wait_recv())

    def corner_up():
        return pltpu.make_async_remote_copy(
            src_ref=halo_in.at[1], dst_ref=halo_in.at[groups + 1],
            send_sem=corner_send.at[0], recv_sem=corner_recv.at[0],
            device_id={"gy": my - 1}, device_id_type=MESH,
        )

    def corner_down():
        return pltpu.make_async_remote_copy(
            src_ref=halo_in.at[groups], dst_ref=halo_in.at[0],
            send_sem=corner_send.at[1], recv_sem=corner_recv.at[1],
            device_id={"gy": my + 1}, device_id_type=MESH,
        )

    pl.when(has_up)(lambda: corner_up().start())
    pl.when(has_down)(lambda: corner_down().start())

    def shift_row(i):
        g = (i - 1 + per) // per
        turn = lax.rem(width - lax.rem(i - 1 + per, per) * depth, width)
        left = pltpu.roll(halo_in[g, 0], turn, 1)
        right = pltpu.roll(halo_in[g, 1], turn, 1)
        for z in range(depth):
            tile = xs[i, z + 1]
            edge = left if z == 0 else pltpu.roll(left, width - z, 1)
            shifted[0, z + 1] = jnp.where(lane == 0, edge, pltpu.roll(tile, 1, 1))
            shifted[1, z + 1] = jnp.where(
                lane == width - 1,
                pltpu.roll(right, width - 1 - z, 1),
                pltpu.roll(tile, width - 1, 1),
            )

    def window(i, d, z):
        at = pl.ds(z, 4)
        tile = xs[i, at] if d == 1 else shifted[d // 2, at]
        return tile.reshape(4 * ch, width)

    def lift_row(i, taps=3):
        shift_row(i)
        for q in range(depth // 4):
            rhs = jnp.concatenate(
                [
                    jnp.concatenate([window(i, d, 4 * q), window(i, d, 4 * q + 2)], axis=1)
                    for d in range(3)
                ],
                axis=0,
            )
            acc = jnp.dot(toep[0:2 * ch * taps], rhs, preferred_element_type=F32)
            if taps == 3:
                y = i - 2
                done = carry_b[q] + acc[4 * ch:6 * ch]
                for p in range(2):
                    own = xs[y + 1, pl.ds(4 * q + 2 * p + 1, 2)].reshape(2 * ch, width)
                    new = (own.astype(F32) + done[:, p * width:(p + 1) * width]).astype(BF16)
                    lifted[y, 2 * q + p] = new
                    modes_part = lax.dot_general(fwd[...], new, NT, preferred_element_type=F32)
                    part[y * pairs + 2 * q + p] = modes_part.astype(BF16)
            if taps >= 2:
                carry_b[q] = carry_a[q] + acc[2 * ch:4 * ch]
            carry_a[q] = acc[0:2 * ch]

    def rs_copy(c, o):
        to = lax.rem(me + o, n)
        return pltpu.make_async_remote_copy(
            src_ref=part.at[pl.ds(c * cpairs + to * share, share)], dst_ref=got.at[c, o],
            send_sem=rs_send.at[c, o], recv_sem=rs_recv.at[c, o],
            device_id={"gx": to}, device_id_type=MESH,
        )

    def ag_copy(c, o):
        mine = pl.ds(c * cpairs + me * share, share)
        return pltpu.make_async_remote_copy(
            src_ref=mixed.at[mine], dst_ref=mixed.at[mine],
            send_sem=ag_send.at[c, o], recv_sem=ag_recv.at[c, o],
            device_id={"gx": lax.rem(me + o, n)}, device_id_type=MESH,
        )

    def ag_wait(c, o):
        theirs = pl.ds(c * cpairs + lax.rem(me + n - o, n) * share, share)
        pltpu.make_async_remote_copy(
            src_ref=mixed.at[theirs], dst_ref=mixed.at[theirs],
            send_sem=ag_send.at[c, o], recv_sem=ag_recv.at[c, o],
            device_id={"gx": lax.rem(me + o, n)}, device_id_type=MESH,
        ).wait_recv()

    def lift_chunk(c):
        pl.loop(c * crows + 2, (c + 1) * crows + 2)(lift_row)
        pl.loop(1, n)(lambda o: rs_copy(c, o).start())

    def mix_chunk(c):
        mine = pl.ds(c * cpairs + me * share, share)
        tsum[...] = part[mine].astype(F32)

        @pl.loop(1, n)
        def _(o):
            rs_copy(c, o).wait_recv()
            tsum[...] += got[c, o].astype(F32)

        for k in range(modes):
            data = jnp.concatenate([tsum[:, k, :], tsum[:, modes + k, :]], axis=1)
            top = data.astype(BF16).astype(F32)
            lhs = jnp.concatenate([top, data - top], axis=0).astype(BF16)
            both = lax.dot_general(lhs, mixw[k], NT, preferred_element_type=F32)
            new = both[0:share] + both[share:2 * share]
            tsum[:, k, :] = new[:, :width]
            tsum[:, modes + k, :] = new[:, width:]
        mixed[mine] = tsum[...].astype(BF16)
        pl.loop(1, n)(lambda o: ag_copy(c, o).start())

    slope = math.sqrt(2.0 / math.pi)
    low = jnp.asarray(slope, BF16)
    cubic = jnp.asarray(slope * 0.044715, BF16)

    def finish_row(y):
        for p in range(pairs):
            spec = mixed[y * pairs + p]
            branch = lax.dot_general(
                jnp.concatenate([spec, spec], axis=0), inv[...], TN, preferred_element_type=F32
            )
            blended = (lifted[y, p].astype(F32) + branch).astype(BF16)
            wide = jnp.concatenate([blended[0:ch], blended[ch:2 * ch]], axis=1)
            h = jnp.dot(up_w[...], wide, preferred_element_type=F32).astype(BF16)
            t = jnp.tanh(h * (low + cubic * (h * h)))
            down = jnp.dot(down_w[...], h + h * t, preferred_element_type=F32)
            res = (wide.astype(F32) + down).astype(BF16)
            out[y, p, 0:ch] = res[:, :width]
            out[y, p, ch:2 * ch] = res[:, width:]

    def finish_chunk(c):
        pl.loop(1, n)(lambda o: ag_wait(c, o))
        pl.loop(c * crows, (c + 1) * crows)(finish_row)

    pl.when(has_up)(lambda: row_down().wait_recv())
    pl.when(has_up)(lambda: corner_down().wait_recv())
    lift_row(0, 1)
    lift_row(1, 2)
    for c in range(CHUNKS - 1):
        lift_chunk(c)
        if c:
            mix_chunk(c - 1)
    pl.when(has_down)(lambda: row_up().wait_recv())
    pl.when(has_down)(lambda: corner_up().wait_recv())
    lift_chunk(CHUNKS - 1)
    mix_chunk(CHUNKS - 2)
    finish_chunk(0)
    mix_chunk(CHUNKS - 1)
    for c in range(1, CHUNKS):
        finish_chunk(c)

    pl.when(has_up)(lambda: row_up().wait_send())
    pl.when(has_down)(lambda: row_down().wait_send())
    pl.when(has_up)(lambda: corner_up().wait_send())
    pl.when(has_down)(lambda: corner_down().wait_send())
    for g in range(groups):
        pl.when(has_left)(lambda g=g: side_left(g).wait_send())
        pl.when(has_right)(lambda g=g: side_right(g).wait_send())
    for c in range(CHUNKS):
        @pl.loop(1, n)
        def _(o):
            rs_copy(c, o).wait_send()
            ag_copy(c, o).wait_send()


def per_device(n, m, field, conv_w, spec_re, spec_im, mlp_in, mlp_out):
    rows, depth, ch, width = field.shape
    modes = spec_re.shape[0]
    pairs = depth // 2
    cpairs = rows // CHUNKS * pairs
    share = cpairs // n
    groups = rows * depth // width
    dma = pltpu.SemaphoreType.DMA
    vmem = pl.BlockSpec(memory_space=pltpu.VMEM)
    result = pl.pallas_call(
        functools.partial(kernel, n, m),
        out_shape=pltpu.VMEM((rows, pairs, 2 * ch, width), BF16),
        in_specs=[pl.BlockSpec(memory_space=pltpu.HBM)] + [vmem] * 5,
        out_specs=vmem,
        scratch_shapes=[
            pltpu.VMEM((rows + 2, depth + 2, ch, width), BF16),
            pltpu.VMEM((2, depth + 2, ch, width), BF16),
            pltpu.VMEM((depth // 4, 2 * ch, 2 * width), F32),
            pltpu.VMEM((depth // 4, 2 * ch, 2 * width), F32),
            pltpu.VMEM((rows, pairs, 2 * ch, width), BF16),
            pltpu.VMEM((2, groups, ch, width), BF16),
            pltpu.VMEM((groups + 2, 2, ch, width), BF16),
            pltpu.VMEM(mlp_in.shape, BF16),
            pltpu.VMEM(mlp_out.shape, BF16),
            pltpu.VMEM((6 * ch, 12 * ch), BF16),
            pltpu.VMEM((modes, 4 * ch, 4 * ch), BF16),
            pltpu.VMEM((2 * modes, width), BF16),
            pltpu.VMEM((4 * modes, width), BF16),
            pltpu.VMEM((rows * pairs, 2 * modes, width), BF16),
            pltpu.VMEM((CHUNKS, n, share, 2 * modes, width), BF16),
            pltpu.VMEM((share, 2 * modes, width), F32),
            pltpu.VMEM((rows * pairs, 2 * modes, width), BF16),
            dma((rows,)),
            dma((2,)), dma((2,)),
            dma((2, groups)), dma((2, groups)),
            dma((2,)), dma((2,)),
            dma((CHUNKS, n)), dma((CHUNKS, n)),
            dma((CHUNKS, n)), dma((CHUNKS, n)),
        ],
        compiler_params=pltpu.CompilerParams(
            collective_id=0, has_side_effects=True, vmem_limit_bytes=40 << 20
        ),
    )(field, conv_w, spec_re, spec_im, mlp_in.T, mlp_out)
    return result.reshape(rows, depth, ch, width)


def solution(mesh):
    in_specs = (P("gy", None, None, "gx"), P(), P(), P(), P(), P())
    out_specs = P("gy", None, None, "gx")
    return jax.shard_map(
        functools.partial(per_device, mesh.shape["gx"], mesh.shape["gy"]),
        mesh=mesh, in_specs=in_specs, out_specs=out_specs, check_vma=False,
    )
```
